128 devices in a mesh: dp: 8 (over x, core), seq: 16 (over y, z).
Axes of the slice: x: 4, y: 4, z: 4, core: 2. Of those that a mesh axis runs over, the one named last changes fastest.
Arguments:
- queries: bfloat16 [16, 98304, 128], P(None, ('dp', 'seq')), parts along dimension 1, may hold values from -6 to 6
- key_rows: bfloat16 [16, 98304, 128], P(None, ('dp', 'seq')), parts along dimension 1, may hold values from -6 to 6
- value_rows: bfloat16 [16, 98304, 128], P(None, ('dp', 'seq')), parts along dimension 1, may hold values from -6 to 6
- out_grad: bfloat16 [16, 98304, 128], P(None, ('dp', 'seq')), parts along dimension 1, may hold values from -6 to 6
Outputs:
- attended: bfloat16 [16, 98304, 128], P(None, ('dp', 'seq')), parts along dimension 1
- grad_queries: bfloat16 [16, 98304, 128], P(None, ('dp', 'seq')), parts along dimension 1
- grad_keys: bfloat16 [16, 98304, 128], P(None, ('dp', 'seq')), parts along dimension 1
- grad_values: bfloat16 [16, 98304, 128], P(None, ('dp', 'seq')), parts along dimension 1
The draws below stay inside these ranges and needn't reach their ends.
There are 8 independent parts, one for each index of `dp`. The reference program is written for one: setup_inputs(seed, part) draws one part's arguments, and reference() takes and returns one part's arrays. A program takes and returns all parts, laid end to end along the dimension named above; each array names one. Nothing has to cross between parts.
All inputs are finite; a program needn't handle non-finite values.
Results may differ from the reference program's by a relative error of at most 0.009.
Values may be sent and summed in bfloat16 or wider, within the bound.
A program may use at most 192 MiB of HBM per device.

```python
import jax
import jax.numpy as jnp
from jax import lax

HEADS = 16
DH = 128
SEQLEN = 12288
N_SEQ = 16


def levels(rng, extent, shards, least, top_value):
    loudness, own = 1.0, jax.random.fold_in(rng, 6)
    for axis_at, shards_of in shards:
        heights = jnp.exp(jax.random.uniform(jax.random.fold_in(own, axis_at), (shards_of,), jnp.float32, least / len(shards), top_value / len(shards)))
        loudness = loudness * jnp.repeat(heights, extent[axis_at] // shards_of).reshape([-1 if axis == axis_at else 1 for axis in range(len(extent))])
    return loudness


def scatter_about(stream_key, extent, scale, bound, cuts=(), kind=jnp.bfloat16):
    values = scale * jax.random.normal(stream_key, extent, jnp.float32)
    if cuts:
        values = values * levels(stream_key, extent, cuts, -0.22, 0.18)
    return jnp.clip(values, -bound, bound).astype(kind)


def setup_inputs(seed: int = 0, part: int = 0) -> dict:
    streams_of = jax.random.split(jax.random.key(seed), 5)
    part_splits = jax.random.split(jax.random.fold_in(streams_of[4], part), 5)
    queries = scatter_about(part_splits[0], (HEADS, SEQLEN, DH), 1.0, 6.0, ((1, 16),))
    key_rows = scatter_about(part_splits[1], (HEADS, SEQLEN, DH), 1.0, 6.0, ((1, 16),))
    value_rows = scatter_about(part_splits[2], (HEADS, SEQLEN, DH), 1.0, 6.0, ((1, 16),))
    out_grad = scatter_about(part_splits[3], (HEADS, SEQLEN, DH), 1.0, 6.0, ((1, 16),))
    return {"queries": queries, "key_rows": key_rows, "value_rows": value_rows, "out_grad": out_grad}


def to_half(values):
    return lax.optimization_barrier(values.astype(jnp.bfloat16))

def block_terms(pieces):
    q_blk, k_blk, v_blk, g_blk, pre_blk, suf_blk = pieces
    wide = jnp.float32
    qf = q_blk.astype(wide)
    kf = k_blk.astype(wide)
    vf = v_blk.astype(wide)
    gf = g_blk.astype(wide)
    pf = pre_blk.astype(wide)
    rf = suf_blk.astype(wide)
    length = q_blk.shape[1]
    rows_idx = jnp.arange(length, dtype=jnp.int32)
    causal = rows_idx[:, None] >= rows_idx[None, :]
    scores = jnp.einsum('htd,hsd->hts', qf, kf)
    masked = to_half(jnp.where(causal[None], scores, 0.0)).astype(wide)
    dots = jnp.einsum('htd,hsd->hts', gf, vf)
    mdots = to_half(jnp.where(causal[None], dots, 0.0)).astype(wide)
    inner = jnp.einsum('hts,hsd->htd', masked, vf) + jnp.einsum('hta,hab->htb', qf, pf)
    dq_full = jnp.einsum('hts,hsd->htd', mdots, kf) + jnp.einsum('htb,hab->hta', gf, pf)
    dk_full = jnp.einsum('hts,htd->hsd', mdots, qf) + jnp.einsum('hsb,hab->hsa', vf, rf)
    dv_full = jnp.einsum('hts,htd->hsd', masked, gf) + jnp.einsum('hsa,hab->hsb', kf, rf)
    return (inner, dq_full, dk_full, dv_full)

def reference(queries, key_rows, value_rows, out_grad):
    wide = jnp.float32
    heads, total, width = queries.shape
    blocks = N_SEQ
    length = total // blocks
    position = jnp.arange(total, dtype=jnp.int32).astype(wide)
    scale = 1.0 / jnp.sqrt(width * (position + 1.0))
    scaled_grad = to_half(scale[None, :, None] * out_grad.astype(wide))

    def split(array):
        return array.reshape(heads, blocks, length, width).transpose(1, 0, 2, 3)
    q_b = split(queries)
    k_b = split(key_rows)
    v_b = split(value_rows)
    g_b = split(scaled_grad)
    key_state = to_half(jnp.einsum('nhta,nhtb->nhab', k_b.astype(wide), v_b.astype(wide)))
    grad_state = to_half(jnp.einsum('nhta,nhtb->nhab', q_b.astype(wide), g_b.astype(wide)))
    zeros = jnp.zeros((1, heads, width, width), wide)
    forward_sum = jnp.cumsum(key_state.astype(wide), axis=0)
    prefix = to_half(jnp.concatenate([zeros, forward_sum[:-1]], axis=0))
    backward_sum = jnp.flip(jnp.cumsum(jnp.flip(grad_state.astype(wide), 0), axis=0), 0)
    suffix = to_half(jnp.concatenate([backward_sum[1:], zeros], axis=0))
    inner, dq_full, dk_full, dv_full = lax.map(block_terms, (q_b, k_b, v_b, g_b, prefix, suffix))

    def join(array):
        return array.transpose(1, 0, 2, 3).reshape(heads, total, width)
    attended = (scale[None, :, None] * join(inner)).astype(jnp.bfloat16)
    return (attended, join(dq_full).astype(jnp.bfloat16), join(dk_full).astype(jnp.bfloat16), join(dv_full).astype(jnp.bfloat16))
```

```python
import functools

import jax
import jax.numpy as jnp
from jax import lax
from jax.experimental import pallas as pl
from jax.experimental.pallas import tpu as pltpu
from jax.sharding import PartitionSpec as P

MESH = pl.DeviceIdType.MESH
WIDE = jnp.float32
HALF = jnp.bfloat16
CHUNK = 256
EARLY = 8


def nn(a, b):
    return lax.dot_general(a, b, (((1,), (0,)), ((), ())), preferred_element_type=WIDE)


def nt(a, b):
    return lax.dot_general(a, b, (((1,), (1,)), ((), ())), preferred_element_type=WIDE)


def tn(a, b):
    return lax.dot_general(a, b, (((0,), (0,)), ((), ())), preferred_element_type=WIDE)


def states_kernel(
    side, q_in, k_in, v_in, g_in,
    q_ref, k_ref, v_ref, g_ref, att_ref, dq_ref, dk_ref, dv_ref, pre_ref, suf_ref, got_ref, scale_ref,
    send1, recv1, send2, in_sem, ss1, rs1, ss2, rs2,
):
    heads, length, width = q_in.shape
    chunks = length // CHUNK
    me = lax.axis_index("seq")
    count = heads

    def loads(h):
        pairs = ((k_in, k_ref), (v_in, v_ref), (q_in, q_ref), (g_in, g_ref))
        return [
            pltpu.make_async_copy(src.at[h], dst.at[h], in_sem.at[h, i])
            for i, (src, dst) in enumerate(pairs)
        ]

    def peer(i):
        row, col = me // side, me % side
        return ((row + i // side) % side) * side + (col + i % side) % side

    @pl.loop(0, count)
    def _(i):
        for copy in loads(peer((i + 1) % count)):
            copy.start()

    barrier = pltpu.get_barrier_semaphore()

    @pl.loop(1, count)
    def _(i):
        pl.semaphore_signal(barrier, inc=1, device_id={"seq": peer(i)}, device_id_type=MESH)

    position = (me * length + lax.broadcasted_iota(jnp.int32, (length, width), 0)).astype(WIDE)
    scale_ref[...] = 1.0 / jnp.sqrt(width * (position + 1.0))
    pl.semaphore_wait(barrier, count - 1)

    def first(h):
        return pltpu.make_async_remote_copy(
            src_ref=send1.at[h], dst_ref=recv1.at[me], send_sem=ss1.at[h], recv_sem=rs1.at[me],
            device_id={"seq": h}, device_id_type=MESH,
        )

    def second(j):
        return pltpu.make_async_remote_copy(
            src_ref=send2.at[j], dst_ref=got_ref.at[me], send_sem=ss2.at[j], recv_sem=rs2.at[me],
            device_id={"seq": j}, device_id_type=MESH,
        )

    def first_from(j):
        return pltpu.make_async_remote_copy(
            src_ref=send1.at[j], dst_ref=recv1.at[j], send_sem=ss1.at[j], recv_sem=rs1.at[j],
            device_id={"seq": j}, device_id_type=MESH,
        )

    def second_from(j):
        return pltpu.make_async_remote_copy(
            src_ref=send2.at[j], dst_ref=got_ref.at[j], send_sem=ss2.at[j], recv_sem=rs2.at[j],
            device_id={"seq": j}, device_id_type=MESH,
        )

    def form_states(h, out):
        for copy in loads(h):
            copy.wait()
        key_sum, grads = None, []
        for c in range(chunks):
            rows = pl.ds(c * CHUNK, CHUNK)
            scaled = (scale_ref[rows, :] * g_ref[h, rows, :].astype(WIDE)).astype(HALF)
            g_ref[h, rows, :] = scaled
            key = tn(k_ref[h, rows, :], v_ref[h, rows, :])
            grads.append(tn(q_ref[h, rows, :], scaled))
            if c:
                pre_ref[h, c - 1] = key_sum
            key_sum = key if c == 0 else key_sum + key
        total = None
        for c in reversed(range(chunks)):
            if c < chunks - 1:
                suf_ref[h, c] = total
            total = grads[c] if total is None else total + grads[c]
        out[0] = key_sum.astype(HALF)
        out[1] = total.astype(HALF)

    @pl.loop(1, count)
    def _(i):
        h = peer(i)
        form_states(h, send1.at[h])
        first(h).start()

    form_states(me, recv1.at[me])

    causal = lax.broadcasted_iota(jnp.int32, (CHUNK, CHUNK), 0) >= lax.broadcasted_iota(
        jnp.int32, (CHUNK, CHUNK), 1
    )

    def inside(h):
        for c in range(chunks):
            rows = pl.ds(c * CHUNK, CHUNK)
            q, k, v, g = q_ref[h, rows, :], k_ref[h, rows, :], v_ref[h, rows, :], g_ref[h, rows, :]
            scores = jnp.where(causal, nt(q, k), 0.0).astype(HALF)
            dots = jnp.where(causal, nt(g, v), 0.0).astype(HALF)
            att_ref[h, rows, :] = nn(scores, v)
            dq_ref[h, rows, :] = nn(dots, k)
            dk_ref[h, rows, :] = tn(dots, q)
            dv_ref[h, rows, :] = tn(scores, g)

    @pl.loop(0, EARLY)
    def _(h):
        inside(h)

    @pl.loop(1, count)
    def _(i):
        first_from(peer(i)).wait_recv()

    total = jnp.zeros((width, width), WIDE)
    for j in range(count):
        send2[j, 0] = total.astype(HALF)
        total = total + recv1[j, 0].astype(WIDE)
    total = jnp.zeros((width, width), WIDE)
    for j in reversed(range(count)):
        send2[j, 1] = total.astype(HALF)
        total = total + recv1[j, 1].astype(WIDE)

    @pl.loop(1, count)
    def _(i):
        second(peer(i)).start()

    got_ref[me] = send2[me]

    @pl.loop(EARLY, heads)
    def _(h):
        inside(h)

    @pl.loop(1, count)
    def _(i):
        second_from(peer(i)).wait_recv()

    @pl.loop(1, count)
    def _(i):
        first(peer(i)).wait_send()
        second(peer(i)).wait_send()


def finish_kernel(
    q_ref, k_ref, v_ref, g_ref, att_in, dq_in, dk_in, dv_in, pre_ref, suf_ref, got_ref, scale_ref,
    att_ref, dq_ref, dk_ref, dv_ref,
):
    h = pl.program_id(0)
    chunks = q_ref.shape[1] // CHUNK
    prefix, suffix = got_ref[h, 0].astype(WIDE), got_ref[h, 1].astype(WIDE)
    for c in range(chunks):
        rows = pl.ds(c * CHUNK, CHUNK)
        before = (prefix + pre_ref[h, c - 1] if c else prefix).astype(HALF)
        after = (suffix + suf_ref[h, c] if c < chunks - 1 else suffix).astype(HALF)
        q, k, v, g = q_ref[h, rows, :], k_ref[h, rows, :], v_ref[h, rows, :], g_ref[h, rows, :]
        att_ref[0, rows, :] = (scale_ref[rows, :] * (att_in[h, rows, :] + nn(q, before))).astype(HALF)
        dq_ref[0, rows, :] = (dq_in[h, rows, :] + nt(g, before)).astype(HALF)
        dk_ref[0, rows, :] = (dk_in[h, rows, :] + nt(v, after)).astype(HALF)
        dv_ref[0, rows, :] = (dv_in[h, rows, :] + nn(k, after)).astype(HALF)


def on_device(side, queries, key_rows, value_rows, out_grad):
    heads, length, width = queries.shape
    chunks = length // CHUNK
    rows = [pltpu.VMEM((heads, length, width), HALF)] * 4
    parts = [pltpu.VMEM((heads, length, width), WIDE)] * 4
    inner = [pltpu.VMEM((heads, chunks - 1, width, width), WIDE)] * 2
    got = [pltpu.VMEM((heads, 2, width, width), HALF)]
    scale = [pltpu.VMEM((length, width), WIDE)]
    vmem = pl.BlockSpec(memory_space=pltpu.VMEM)
    held = pl.pallas_call(
        functools.partial(states_kernel, side),
        out_shape=rows + parts + inner + got + scale,
        in_specs=[pl.BlockSpec(memory_space=pl.ANY)] * 4,
        out_specs=[vmem] * 12,
        scratch_shapes=[
            pltpu.VMEM((heads, 2, width, width), HALF),
            pltpu.VMEM((heads, 2, width, width), HALF),
            pltpu.VMEM((heads, 2, width, width), HALF),
            pltpu.SemaphoreType.DMA((heads, 4)),
            pltpu.SemaphoreType.DMA((heads,)),
            pltpu.SemaphoreType.DMA((heads,)),
            pltpu.SemaphoreType.DMA((heads,)),
            pltpu.SemaphoreType.DMA((heads,)),
        ],
        compiler_params=pltpu.CompilerParams(collective_id=0, has_side_effects=True, vmem_limit_bytes=12 * 2**20),
        name="states",
    )(queries, key_rows, value_rows, out_grad)
    block = pl.BlockSpec((1, length, width), lambda h: (h, 0, 0))
    return pl.pallas_call(
        finish_kernel,
        grid=(heads,),
        out_shape=[jax.ShapeDtypeStruct((heads, length, width), HALF)] * 4,
        in_specs=[vmem] * 12,
        out_specs=[block] * 4,
        compiler_params=pltpu.CompilerParams(vmem_limit_bytes=12 * 2**20),
        name="finish",
    )(*held)


def solution(mesh):
    side = 4
    placed = P(None, ("dp", "seq"), None)
    return jax.shard_map(
        functools.partial(on_device, side),
        mesh=mesh,
        in_specs=(placed,) * 4,
        out_specs=(placed,) * 4,
        check_vma=False,
    )
```

```python
import functools

import jax
import jax.numpy as jnp
from jax import lax
from jax.experimental import pallas as pl
from jax.experimental.pallas import tpu as pltpu
from jax.sharding import PartitionSpec as P

MESH = pl.DeviceIdType.MESH
WIDE = jnp.float32
HALF = jnp.bfloat16
CHUNK = 256
EARLY, MIDDLE = 3, 7
TOGETHER, SLOTS = 2, 4


def nn(a, b):
    return lax.dot_general(a, b, (((1,), (0,)), ((), ())), preferred_element_type=WIDE)


def nt(a, b):
    return lax.dot_general(a, b, (((1,), (1,)), ((), ())), preferred_element_type=WIDE)


def tn(a, b):
    return lax.dot_general(a, b, (((0,), (0,)), ((), ())), preferred_element_type=WIDE)


def states_kernel(
    side, q_in, k_in, v_in, g_in,
    q_ref, k_ref, v_ref, g_ref, att_ref, dq_ref, dk_ref, dv_ref, pre_ref, suf_ref, got_ref, scale_ref,
    sent, taken, back, in_sem, send_sem, recv_sem,
):
    heads, length, width = q_in.shape
    chunks = length // CHUNK
    me = lax.axis_index("seq")
    row, col = me // side, me % side
    count = heads
    others = [(dy, dz) for dy in range(side) for dz in range(side) if dy or dz]

    def base(dy):
        return ((row + dy) % side) * side

    def peer(dy, dz):
        return base(dy) + (col + dz) % side

    def loads(dy, kind):
        pairs = (((k_in, k_ref), (v_in, v_ref)), ((q_in, q_ref), (g_in, g_ref)))[kind]
        group = pl.ds(base(dy), side)
        return [
            pltpu.make_async_copy(src.at[group], dst.at[group], in_sem.at[kind, i, dy])
            for i, (src, dst) in enumerate(pairs)
        ]

    def gather(kind, h):
        return pltpu.make_async_remote_copy(
            src_ref=sent.at[kind, h], dst_ref=taken.at[kind, me],
            send_sem=send_sem.at[0, kind], recv_sem=recv_sem.at[0, kind],
            device_id={"seq": h}, device_id_type=MESH,
        )

    def scatter(kind, j):
        return pltpu.make_async_remote_copy(
            src_ref=back.at[kind, j], dst_ref=got_ref.at[kind, me],
            send_sem=send_sem.at[1, kind], recv_sem=recv_sem.at[1, kind],
            device_id={"seq": j}, device_id_type=MESH,
        )

    def all_of(stage, kind):
        many = pl.ds(0, count - 1)
        return pltpu.make_async_remote_copy(
            src_ref=(sent, back)[stage].at[kind, many], dst_ref=(taken, got_ref)[stage].at[kind, many],
            send_sem=send_sem.at[stage, kind], recv_sem=recv_sem.at[stage, kind],
            device_id={"seq": peer(0, 1)}, device_id_type=MESH,
        )

    order = [*range(1, side), 0]
    for dy in order:
        for copy in loads(dy, 0):
            copy.start()

    barrier = pltpu.get_barrier_semaphore()
    for dy, dz in others:
        pl.semaphore_signal(barrier, inc=1, device_id={"seq": peer(dy, dz)}, device_id_type=MESH)

    for dy in order:
        for copy in loads(dy, 1):
            copy.start()

    position = (me * length + lax.broadcasted_iota(jnp.int32, (length, width), 0)).astype(WIDE)
    scale_ref[...] = 1.0 / jnp.sqrt(width * (position + 1.0))

    def key_state(h):
        total = None
        for c in range(chunks):
            rows = pl.ds(c * CHUNK, CHUNK)
            if c:
                pre_ref[h, c - 1] = total
            part = tn(k_ref[h, rows, :], v_ref[h, rows, :])
            total = part if total is None else total + part
        sent[0, h] = total.astype(HALF)

    def grad_state(h):
        total = None
        for c in reversed(range(chunks)):
            rows = pl.ds(c * CHUNK, CHUNK)
            scaled = (scale_ref[rows, :] * g_ref[h, rows, :].astype(WIDE)).astype(HALF)
            g_ref[h, rows, :] = scaled
            if c < chunks - 1:
                suf_ref[h, c] = total
            part = tn(q_ref[h, rows, :], scaled)
            total = part if total is None else total + part
        sent[1, h] = total.astype(HALF)

    for kind in range(2):

        @pl.loop(0, side)
        def _(t):
            dy = (t + 1) % side
            for copy in loads(dy, kind):
                copy.wait()

            @pl.when(t > 0)
            def _():
                if kind == 0:

                    @pl.when(t == 1)
                    def _():
                        pl.semaphore_wait(barrier, count - 1)

                for dz in range(side):
                    gather(kind, peer(t, dz)).start()

            for dz in range(side):
                (key_state, grad_state)[kind](peer(dy, dz))

        taken[kind, me] = sent[kind, me]
        for dz in range(1, side):
            gather(kind, peer(0, dz)).start()

    causal = lax.broadcasted_iota(jnp.int32, (CHUNK, CHUNK), 0) >= lax.broadcasted_iota(
        jnp.int32, (CHUNK, CHUNK), 1
    )

    def inside(start, stop):
        @pl.loop(start, stop)
        def _(h):
            for c in range(chunks):
                rows = pl.ds(c * CHUNK, CHUNK)
                q, k, v, g = q_ref[h, rows, :], k_ref[h, rows, :], v_ref[h, rows, :], g_ref[h, rows, :]
                scores = jnp.where(causal, nt(q, k), 0.0).astype(HALF)
                dots = jnp.where(causal, nt(g, v), 0.0).astype(HALF)
                att_ref[h, rows, :] = nn(scores, v)
                dq_ref[h, rows, :] = nn(dots, k)
                dk_ref[h, rows, :] = tn(dots, q)
                dv_ref[h, rows, :] = tn(scores, g)

    def give_back(kind):
        all_of(0, kind).wait_recv()
        total = jnp.zeros((width, width), WIDE)
        for j in range(count) if kind == 0 else reversed(range(count)):
            back[kind, j] = total.astype(HALF)
            total = total + taken[kind, j].astype(WIDE)
        for dy, dz in others:
            scatter(kind, peer(dy, dz)).start()
        got_ref[kind, me] = back[kind, me]

    inside(0, EARLY)
    give_back(0)
    inside(EARLY, MIDDLE)
    give_back(1)
    inside(MIDDLE, heads)
    for kind in range(2):
        all_of(1, kind).wait_recv()
        for stage in range(2):
            all_of(stage, kind).wait_send()


def finish_kernel(
    q_ref, k_ref, v_ref, g_ref, att_in, dq_in, dk_in, dv_in, pre_ref, suf_ref, got_ref, scale_ref,
    att_out, dq_out, dk_out, dv_out, att_ref, dq_ref, dk_ref, dv_ref, out_sem,
):
    heads, length, _ = q_ref.shape
    chunks = length // CHUNK

    def stores(h):
        pairs = ((att_ref, att_out), (dq_ref, dq_out), (dk_ref, dk_out), (dv_ref, dv_out))
        return [
            pltpu.make_async_copy(src.at[h % SLOTS], dst.at[h], out_sem.at[i, h % SLOTS])
            for i, (src, dst) in enumerate(pairs)
        ]

    def finish(h):
        slot = h % SLOTS
        prefix, suffix = got_ref[0, h].astype(WIDE), got_ref[1, h].astype(WIDE)
        for c in range(chunks):
            rows = pl.ds(c * CHUNK, CHUNK)
            before = (prefix + pre_ref[h, c - 1] if c else prefix).astype(HALF)
            after = (suffix + suf_ref[h, c] if c < chunks - 1 else suffix).astype(HALF)
            q, k, v, g = q_ref[h, rows, :], k_ref[h, rows, :], v_ref[h, rows, :], g_ref[h, rows, :]
            att_ref[slot, rows, :] = (scale_ref[rows, :] * (att_in[h, rows, :] + nn(q, before))).astype(HALF)
            dq_ref[slot, rows, :] = (dq_in[h, rows, :] + nt(g, before)).astype(HALF)
            dk_ref[slot, rows, :] = (dk_in[h, rows, :] + nt(v, after)).astype(HALF)
            dv_ref[slot, rows, :] = (dv_in[h, rows, :] + nn(k, after)).astype(HALF)

    @pl.loop(0, heads // TOGETHER)
    def _(i):
        @pl.when(i >= SLOTS // TOGETHER)
        def _():
            for b in range(TOGETHER):
                for copy in stores(i * TOGETHER + b - SLOTS):
                    copy.wait()

        for b in range(TOGETHER):
            finish(i * TOGETHER + b)
        for b in range(TOGETHER):
            for copy in stores(i * TOGETHER + b):
                copy.start()

    @pl.loop(heads - SLOTS, heads)
    def _(h):
        for copy in stores(h):
            copy.wait()


def on_device(side, queries, key_rows, value_rows, out_grad):
    heads, length, width = queries.shape
    chunks = length // CHUNK
    rows = [pltpu.VMEM((heads, length, width), HALF)] * 4
    parts = [pltpu.VMEM((heads, length, width), WIDE)] * 4
    inner = [pltpu.VMEM((heads, chunks - 1, width, width), WIDE)] * 2
    got = [pltpu.VMEM((2, heads, width, width), HALF)]
    scale = [pltpu.VMEM((length, width), WIDE)]
    vmem = pl.BlockSpec(memory_space=pltpu.VMEM)
    hbm = pl.BlockSpec(memory_space=pl.ANY)
    held = pl.pallas_call(
        functools.partial(states_kernel, side),
        out_shape=rows + parts + inner + got + scale,
        in_specs=[hbm] * 4,
        out_specs=[vmem] * 12,
        scratch_shapes=[pltpu.VMEM((2, heads, width, width), HALF)] * 3
        + [
            pltpu.SemaphoreType.DMA((2, 2, side)),
            pltpu.SemaphoreType.DMA((2, 2)),
            pltpu.SemaphoreType.DMA((2, 2)),
        ],
        compiler_params=pltpu.CompilerParams(collective_id=0, has_side_effects=True, vmem_limit_bytes=12 * 2**20),
        name="states",
    )(queries, key_rows, value_rows, out_grad)
    return pl.pallas_call(
        finish_kernel,
        out_shape=[jax.ShapeDtypeStruct((heads, length, width), HALF)] * 4,
        in_specs=[vmem] * 12,
        out_specs=[hbm] * 4,
        scratch_shapes=[pltpu.VMEM((SLOTS, length, width), HALF)] * 4 + [pltpu.SemaphoreType.DMA((4, SLOTS))],
        compiler_params=pltpu.CompilerParams(vmem_limit_bytes=12 * 2**20),
        name="finish",
    )(*held)


def solution(mesh):
    side = 4
    placed = P(None, ("dp", "seq"), None)
    return jax.shard_map(
        functools.partial(on_device, side),
        mesh=mesh,
        in_specs=(placed,) * 4,
        out_specs=(placed,) * 4,
        check_vma=False,
    )
```

```python
import functools

import jax
import jax.numpy as jnp
from jax import lax
from jax.experimental import pallas as pl
from jax.experimental.pallas import tpu as pltpu
from jax.sharding import PartitionSpec as P

MESH = pl.DeviceIdType.MESH
WIDE = jnp.float32
HALF = jnp.bfloat16
CHUNK = 256
EARLY, MIDDLE = 5, 10
TOGETHER, SLOTS = 2, 16


def nn(a, b):
    return lax.dot_general(a, b, (((1,), (0,)), ((), ())), preferred_element_type=WIDE)


def nt(a, b):
    return lax.dot_general(a, b, (((1,), (1,)), ((), ())), preferred_element_type=WIDE)


def tn(a, b):
    return lax.dot_general(a, b, (((0,), (0,)), ((), ())), preferred_element_type=WIDE)


def states_kernel(
    side, q_in, k_in, v_in, g_in,
    k_ref, v_ref, att_ref, dq_ref, dk_ref, dv_ref, suf_ref, after_ref,
    q_ref, g_ref, att_part, dq_part, pre_ref, before_ref, scale_ref,
    sent, taken, back, in_sem, send_sem, recv_sem,
):
    heads, length, width = q_in.shape
    chunks = length // CHUNK
    me = lax.axis_index("seq")
    row, col = me // side, me % side
    count = heads
    got = (before_ref, after_ref)
    others = [(dy, dz) for dy in range(side) for dz in range(side) if dy or dz]

    def base(dy):
        return ((row + dy) % side) * side

    def peer(dy, dz):
        return base(dy) + (col + dz) % side

    def loads(dy, kind):
        pairs = (((k_in, k_ref), (v_in, v_ref)), ((q_in, q_ref), (g_in, g_ref)))[kind]
        group = pl.ds(base(dy), side)
        return [
            pltpu.make_async_copy(src.at[group], dst.at[group], in_sem.at[kind, i, dy])
            for i, (src, dst) in enumerate(pairs)
        ]

    def gather(kind, h):
        return pltpu.make_async_remote_copy(
            src_ref=sent.at[kind, h], dst_ref=taken.at[kind, me],
            send_sem=send_sem.at[0, kind], recv_sem=recv_sem.at[0, kind],
            device_id={"seq": h}, device_id_type=MESH,
        )

    def scatter(kind, j):
        return pltpu.make_async_remote_copy(
            src_ref=back.at[kind, j], dst_ref=got[kind].at[me],
            send_sem=send_sem.at[1, kind], recv_sem=recv_sem.at[1, kind],
            device_id={"seq": j}, device_id_type=MESH,
        )

    def all_of(stage, kind):
        many = pl.ds(0, count - 1)
        return pltpu.make_async_remote_copy(
            src_ref=(sent, back)[stage].at[kind, many],
            dst_ref=got[kind].at[many] if stage else taken.at[kind, many],
            send_sem=send_sem.at[stage, kind], recv_sem=recv_sem.at[stage, kind],
            device_id={"seq": peer(0, 1)}, device_id_type=MESH,
        )

    order = [*range(1, side), 0]
    for dy in order:
        for copy in loads(dy, 0):
            copy.start()

    barrier = pltpu.get_barrier_semaphore()
    for dy, dz in others:
        pl.semaphore_signal(barrier, inc=1, device_id={"seq": peer(dy, dz)}, device_id_type=MESH)

    for dy in order:
        for copy in loads(dy, 1):
            copy.start()

    position = (me * length + lax.broadcasted_iota(jnp.int32, (length, width), 0)).astype(WIDE)
    scale_ref[...] = 1.0 / jnp.sqrt(width * (position + 1.0))

    def key_state(h):
        total = None
        for c in range(chunks):
            rows = pl.ds(c * CHUNK, CHUNK)
            if c:
                pre_ref[h, c - 1] = total
            part = tn(k_ref[h, rows, :], v_ref[h, rows, :])
            total = part if total is None else total + part
        sent[0, h] = total.astype(HALF)

    def grad_state(h):
        total = None
        for c in reversed(range(chunks)):
            rows = pl.ds(c * CHUNK, CHUNK)
            scaled = (scale_ref[rows, :] * g_ref[h, rows, :].astype(WIDE)).astype(HALF)
            g_ref[h, rows, :] = scaled
            if c < chunks - 1:
                suf_ref[h, c] = total
            part = tn(q_ref[h, rows, :], scaled)
            total = part if total is None else total + part
        sent[1, h] = total.astype(HALF)

    for kind in range(2):

        @pl.loop(0, side)
        def _(t):
            dy = (t + 1) % side
            for copy in loads(dy, kind):
                copy.wait()

            @pl.when(t > 0)
            def _():
                if kind == 0:

                    @pl.when(t == 1)
                    def _():
                        pl.semaphore_wait(barrier, count - 1)

                for dz in range(side):
                    gather(kind, peer(t, dz)).start()

            for dz in range(side):
                (key_state, grad_state)[kind](peer(dy, dz))

        taken[kind, me] = sent[kind, me]
        for dz in range(1, side):
            gather(kind, peer(0, dz)).start()

    causal = lax.broadcasted_iota(jnp.int32, (CHUNK, CHUNK), 0) >= lax.broadcasted_iota(
        jnp.int32, (CHUNK, CHUNK), 1
    )

    def inside(start, stop):
        @pl.loop(start, stop)
        def _(h):
            def load(c):
                rows = pl.ds(c * CHUNK, CHUNK)
                return q_ref[h, rows, :], k_ref[h, rows, :], v_ref[h, rows, :], g_ref[h, rows, :]

            def weigh(c):
                q, k, v, g = load(c)
                return (
                    jnp.where(causal, nt(q, k), 0.0).astype(HALF), jnp.where(causal, nt(g, v), 0.0).astype(HALF)
                )

            def apply(c, scores, dots):
                rows = pl.ds(c * CHUNK, CHUNK)
                q, k, v, g = load(c)
                hf = CHUNK // 2
                top, low = pl.ds(c * CHUNK, hf), pl.ds(c * CHUNK + hf, hf)
                att_part[h, top, :] = nn(scores[:hf, :hf], v[:hf])
                att_part[h, low, :] = nn(scores[hf:], v)
                dq_part[h, top, :] = nn(dots[:hf, :hf], k[:hf])
                dq_part[h, low, :] = nn(dots[hf:], k)
                dk_ref[h, top, :] = tn(dots[:, :hf], q)
                dk_ref[h, low, :] = tn(dots[hf:, hf:], q[hf:])
                dv_ref[h, top, :] = tn(scores[:, :hf], g)
                dv_ref[h, low, :] = tn(scores[hf:, hf:], g[hf:])

            held = [weigh(c) for c in range(chunks)]
            for c in range(chunks):
                apply(c, *held[c])

    def give_back(kind):
        all_of(0, kind).wait_recv()
        total = jnp.zeros((width, width), WIDE)
        for j in range(count) if kind == 0 else reversed(range(count)):
            back[kind, j] = total.astype(HALF)
            total = total + taken[kind, j].astype(WIDE)
        for dy, dz in others:
            scatter(kind, peer(dy, dz)).start()
        got[kind][me] = back[kind, me]

    def finish(h):
        prefix = before_ref[h].astype(WIDE)
        for c in range(chunks):
            rows = pl.ds(c * CHUNK, CHUNK)
            before = (prefix + pre_ref[h, c - 1] if c else prefix).astype(HALF)
            q, g = q_ref[h, rows, :], g_ref[h, rows, :]
            att_ref[h, rows, :] = (scale_ref[rows, :] * (att_part[h, rows, :] + nn(q, before))).astype(HALF)
            dq_ref[h, rows, :] = (dq_part[h, rows, :] + nt(g, before)).astype(HALF)

    inside(0, EARLY)
    give_back(0)
    inside(EARLY, MIDDLE)
    give_back(1)
    inside(MIDDLE, heads)
    all_of(1, 0).wait_recv()

    @pl.loop(0, heads // TOGETHER)
    def _(i):
        for b in range(TOGETHER):
            finish(i * TOGETHER + b)

    all_of(1, 1).wait_recv()
    for kind in range(2):
        for stage in range(2):
            all_of(stage, kind).wait_send()


def finish_kernel(
    k_ref, v_ref, att_ref, dq_ref, dk_part, dv_part, suf_ref, after_ref,
    att_out, dq_out, dk_out, dv_out, dk_ref, dv_ref, whole_sem, out_sem,
):
    heads, length, _ = k_ref.shape
    chunks = length // CHUNK
    wholes = [
        pltpu.make_async_copy(src, dst, whole_sem.at[i])
        for i, (src, dst) in enumerate(((att_ref, att_out), (dq_ref, dq_out)))
    ]
    for copy in wholes:
        copy.start()

    def stores(h):
        return [
            pltpu.make_async_copy(src.at[h % SLOTS], dst.at[h], out_sem.at[i, h % SLOTS])
            for i, (src, dst) in enumerate(((dk_ref, dk_out), (dv_ref, dv_out)))
        ]

    def finish(h):
        slot = h % SLOTS
        suffix = after_ref[h].astype(WIDE)
        for c in range(chunks):
            rows = pl.ds(c * CHUNK, CHUNK)
            after = (suffix + suf_ref[h, c] if c < chunks - 1 else suffix).astype(HALF)
            k, v = k_ref[h, rows, :], v_ref[h, rows, :]
            dk_ref[slot, rows, :] = (dk_part[h, rows, :] + nt(v, after)).astype(HALF)
            dv_ref[slot, rows, :] = (dv_part[h, rows, :] + nn(k, after)).astype(HALF)

    @pl.loop(0, heads // TOGETHER)
    def _(i):
        @pl.when(i >= SLOTS // TOGETHER)
        def _():
            for b in range(TOGETHER):
                for copy in stores(i * TOGETHER + b - SLOTS):
                    copy.wait()

        for b in range(TOGETHER):
            finish(i * TOGETHER + b)
        for b in range(TOGETHER):
            for copy in stores(i * TOGETHER + b):
                copy.start()

    @pl.loop(heads - SLOTS, heads)
    def _(h):
        for copy in stores(h):
            copy.wait()

    for copy in wholes:
        copy.wait()


def on_device(side, queries, key_rows, value_rows, out_grad):
    heads, length, width = queries.shape
    chunks = length // CHUNK
    row = pltpu.VMEM((heads, length, width), HALF)
    part = pltpu.VMEM((heads, length, width), WIDE)
    inner = pltpu.VMEM((heads, chunks - 1, width, width), WIDE)
    state = pltpu.VMEM((heads, width, width), HALF)
    vmem = pl.BlockSpec(memory_space=pltpu.VMEM)
    hbm = pl.BlockSpec(memory_space=pl.ANY)
    held = pl.pallas_call(
        functools.partial(states_kernel, side),
        out_shape=[row] * 4 + [part] * 2 + [inner, state],
        in_specs=[hbm] * 4,
        out_specs=[vmem] * 8,
        scratch_shapes=[row] * 2
        + [part] * 2
        + [inner, state, pltpu.VMEM((length, width), WIDE)]
        + [pltpu.VMEM((2, heads, width, width), HALF)] * 3
        + [
            pltpu.SemaphoreType.DMA((2, 2, side)),
            pltpu.SemaphoreType.DMA((2, 2)),
            pltpu.SemaphoreType.DMA((2, 2)),
        ],
        compiler_params=pltpu.CompilerParams(collective_id=0, has_side_effects=True, vmem_limit_bytes=26 * 2**20),
        name="states",
    )(queries, key_rows, value_rows, out_grad)
    return pl.pallas_call(
        finish_kernel,
        out_shape=[jax.ShapeDtypeStruct((heads, length, width), HALF)] * 4,
        in_specs=[vmem] * 8,
        out_specs=[hbm] * 4,
        scratch_shapes=[pltpu.VMEM((SLOTS, length, width), HALF)] * 2
        + [pltpu.SemaphoreType.DMA((2,)), pltpu.SemaphoreType.DMA((2, SLOTS))],
        compiler_params=pltpu.CompilerParams(vmem_limit_bytes=8 * 2**20),
        name="finish",
    )(*held)


def solution(mesh):
    side = 4
    placed = P(None, ("dp", "seq"), None)
    return jax.shard_map(
        functools.partial(on_device, side),
        mesh=mesh,
        in_specs=(placed,) * 4,
        out_specs=(placed,) * 4,
        check_vma=False,
    )
```

```python
import functools

import jax
import jax.numpy as jnp
from jax import lax
from jax.experimental import pallas as pl
from jax.experimental.pallas import tpu as pltpu
from jax.sharding import PartitionSpec as P

MESH = pl.DeviceIdType.MESH
WIDE = jnp.float32
HALF = jnp.bfloat16
CHUNK = 256
EARLY, MIDDLE = 5, 10
TOGETHER, SLOTS = 2, 16


def nn(a, b):
    return lax.dot_general(a, b, (((1,), (0,)), ((), ())), preferred_element_type=WIDE)


def nt(a, b):
    return lax.dot_general(a, b, (((1,), (1,)), ((), ())), preferred_element_type=WIDE)


def tn(a, b):
    return lax.dot_general(a, b, (((0,), (0,)), ((), ())), preferred_element_type=WIDE)


def states_kernel(
    side, q_in, k_in, v_in, g_in,
    k_ref, v_ref, att_ref, dq_ref, dk_ref, dv_ref, suf_ref, after_ref,
    q_ref, g_ref, att_part, dq_part, pre_ref, before_ref, scale_ref,
    sent, taken, back, in_sem, send_sem, recv_sem,
):
    heads, length, width = q_in.shape
    chunks = length // CHUNK
    me = lax.axis_index("seq")
    row, col = me // side, me % side
    count = heads
    got = (before_ref, after_ref)
    others = [(dy, dz) for dy in range(side) for dz in range(side) if dy or dz]

    def base(dy):
        return ((row + dy) % side) * side

    def peer(dy, dz):
        return base(dy) + (col + dz) % side

    def loads(dy, kind):
        pairs = (((k_in, k_ref), (v_in, v_ref)), ((q_in, q_ref), (g_in, g_ref)))[kind]
        group = pl.ds(base(dy), side)
        return [
            pltpu.make_async_copy(src.at[group], dst.at[group], in_sem.at[kind, i, dy])
            for i, (src, dst) in enumerate(pairs)
        ]

    def gather(kind, h):
        return pltpu.make_async_remote_copy(
            src_ref=sent.at[kind, h], dst_ref=taken.at[kind, me],
            send_sem=send_sem.at[0, kind], recv_sem=recv_sem.at[0, kind],
            device_id={"seq": h}, device_id_type=MESH,
        )

    def scatter(kind, j):
        return pltpu.make_async_remote_copy(
            src_ref=back.at[kind, j], dst_ref=got[kind].at[me],
            send_sem=send_sem.at[1, kind], recv_sem=recv_sem.at[1, kind],
            device_id={"seq": j}, device_id_type=MESH,
        )

    unused = (count - 1, 0)
    unneeded = (0, count - 1)

    def all_of(stage, kind, blocks=count - 1):
        many = pl.ds(0, blocks)
        return pltpu.make_async_remote_copy(
            src_ref=(sent, back)[stage].at[kind, many],
            dst_ref=got[kind].at[many] if stage else taken.at[kind, many],
            send_sem=send_sem.at[stage, kind], recv_sem=recv_sem.at[stage, kind],
            device_id={"seq": peer(0, 1)}, device_id_type=MESH,
        )

    order = [*range(1, side), 0]
    for dy in order:
        for copy in loads(dy, 0):
            copy.start()

    barrier = pltpu.get_barrier_semaphore()
    for dy, dz in others:
        pl.semaphore_signal(barrier, inc=1, device_id={"seq": peer(dy, dz)}, device_id_type=MESH)

    for dy in order:
        for copy in loads(dy, 1):
            copy.start()

    position = (me * length + lax.broadcasted_iota(jnp.int32, (length, width), 0)).astype(WIDE)
    scale_ref[...] = 1.0 / jnp.sqrt(width * (position + 1.0))

    def key_state(h):
        total = None
        for c in range(chunks):
            rows = pl.ds(c * CHUNK, CHUNK)
            if c:
                pre_ref[h, c - 1] = total
            part = tn(k_ref[h, rows, :], v_ref[h, rows, :])
            total = part if total is None else total + part
        sent[0, h] = total.astype(HALF)

    def grad_state(h):
        total = None
        for c in reversed(range(chunks)):
            rows = pl.ds(c * CHUNK, CHUNK)
            scaled = (scale_ref[rows, :] * g_ref[h, rows, :].astype(WIDE)).astype(HALF)
            g_ref[h, rows, :] = scaled
            if c < chunks - 1:
                suf_ref[h, c] = total
            part = tn(q_ref[h, rows, :], scaled)
            total = part if total is None else total + part
        sent[1, h] = total.astype(HALF)

    for kind in range(2):

        @pl.loop(0, side)
        def _(t):
            dy = (t + 1) % side
            for copy in loads(dy, kind):
                copy.wait()

            @pl.when(t > 0)
            def _():
                if kind == 0:

                    @pl.when(t == 1)
                    def _():
                        pl.semaphore_wait(barrier, count - 1)

                @pl.when(me != unused[kind])
                def _():
                    for dz in range(side):
                        gather(kind, peer(t, dz)).start()

            for dz in range(side):
                (key_state, grad_state)[kind](peer(dy, dz))

        taken[kind, me] = sent[kind, me]

        @pl.when(me != unused[kind])
        def _():
            for dz in range(1, side):
                gather(kind, peer(0, dz)).start()

    causal = lax.broadcasted_iota(jnp.int32, (CHUNK, CHUNK), 0) >= lax.broadcasted_iota(
        jnp.int32, (CHUNK, CHUNK), 1
    )

    def inside(start, stop):
        @pl.loop(start, stop)
        def _(h):
            def load(c):
                rows = pl.ds(c * CHUNK, CHUNK)
                return q_ref[h, rows, :], k_ref[h, rows, :], v_ref[h, rows, :], g_ref[h, rows, :]

            def weigh(c):
                q, k, v, g = load(c)
                return (
                    jnp.where(causal, nt(q, k), 0.0).astype(HALF), jnp.where(causal, nt(g, v), 0.0).astype(HALF)
                )

            def apply(c, scores, dots):
                rows = pl.ds(c * CHUNK, CHUNK)
                q, k, v, g = load(c)
                hf = CHUNK // 2
                top, low = pl.ds(c * CHUNK, hf), pl.ds(c * CHUNK + hf, hf)
                att_part[h, top, :] = nn(scores[:hf, :hf], v[:hf])
                att_part[h, low, :] = nn(scores[hf:], v)
                dq_part[h, top, :] = nn(dots[:hf, :hf], k[:hf])
                dq_part[h, low, :] = nn(dots[hf:], k)
                dk_ref[h, top, :] = tn(dots[:, :hf], q)
                dk_ref[h, low, :] = tn(dots[hf:, hf:], q[hf:])
                dv_ref[h, top, :] = tn(scores[:, :hf], g)
                dv_ref[h, low, :] = tn(scores[hf:, hf:], g[hf:])

            held = [weigh(c) for c in range(chunks)]
            for c in range(chunks):
                apply(c, *held[c])

    def give_back(kind):
        @pl.when(me == unused[kind])
        def _():
            all_of(0, kind).wait_recv()

        @pl.when(me != unused[kind])
        def _():
            all_of(0, kind, count - 2).wait_recv()

        total = jnp.zeros((width, width), WIDE)
        for j in range(count) if kind == 0 else reversed(range(count)):
            back[kind, j] = total.astype(HALF)
            if j != unused[kind]:
                total = total + taken[kind, j].astype(WIDE)
        for dy, dz in others:

            @pl.when(peer(dy, dz) != unneeded[kind])
            def _():
                scatter(kind, peer(dy, dz)).start()

        got[kind][me] = back[kind, me]

        @pl.when(me == unneeded[kind])
        def _():
            got[kind][...] = jnp.zeros((heads, width, width), HALF)

    def finish(h):
        prefix = before_ref[h].astype(WIDE)
        for c in range(chunks):
            rows = pl.ds(c * CHUNK, CHUNK)
            before = (prefix + pre_ref[h, c - 1] if c else prefix).astype(HALF)
            q, g = q_ref[h, rows, :], g_ref[h, rows, :]
            att_ref[h, rows, :] = (scale_ref[rows, :] * (att_part[h, rows, :] + nn(q, before))).astype(HALF)
            dq_ref[h, rows, :] = (dq_part[h, rows, :] + nt(g, before)).astype(HALF)

    def take(kind):
        @pl.when(me != unneeded[kind])
        def _():
            all_of(1, kind).wait_recv()

    inside(0, EARLY)
    give_back(0)
    inside(EARLY, MIDDLE)
    give_back(1)
    inside(MIDDLE, heads)
    take(0)

    @pl.loop(0, heads // TOGETHER)
    def _(i):
        for b in range(TOGETHER):
            finish(i * TOGETHER + b)

    take(1)
    for kind in range(2):

        @pl.when(me != unused[kind])
        def _():
            all_of(0, kind).wait_send()

        @pl.when(me == unneeded[kind])
        def _():
            all_of(1, kind).wait_send()

        @pl.when(me != unneeded[kind])
        def _():
            all_of(1, kind, count - 2).wait_send()


def finish_kernel(
    k_ref, v_ref, att_ref, dq_ref, dk_part, dv_part, suf_ref, after_ref,
    att_out, dq_out, dk_out, dv_out, dk_ref, dv_ref, whole_sem, out_sem,
):
    heads, length, _ = k_ref.shape
    chunks = length // CHUNK
    wholes = [
        pltpu.make_async_copy(src, dst, whole_sem.at[i])
        for i, (src, dst) in enumerate(((att_ref, att_out), (dq_ref, dq_out)))
    ]
    for copy in wholes:
        copy.start()

    def stores(h):
        return [
            pltpu.make_async_copy(src.at[h % SLOTS], dst.at[h], out_sem.at[i, h % SLOTS])
            for i, (src, dst) in enumerate(((dk_ref, dk_out), (dv_ref, dv_out)))
        ]

    def finish(h):
        slot = h % SLOTS
        suffix = after_ref[h].astype(WIDE)
        for c in range(chunks):
            rows = pl.ds(c * CHUNK, CHUNK)
            after = (suffix + suf_ref[h, c] if c < chunks - 1 else suffix).astype(HALF)
            k, v = k_ref[h, rows, :], v_ref[h, rows, :]
            dk_ref[slot, rows, :] = (dk_part[h, rows, :] + nt(v, after)).astype(HALF)
            dv_ref[slot, rows, :] = (dv_part[h, rows, :] + nn(k, after)).astype(HALF)

    @pl.loop(0, heads // TOGETHER)
    def _(i):
        @pl.when(i >= SLOTS // TOGETHER)
        def _():
            for b in range(TOGETHER):
                for copy in stores(i * TOGETHER + b - SLOTS):
                    copy.wait()

        for b in range(TOGETHER):
            finish(i * TOGETHER + b)
        for b in range(TOGETHER):
            for copy in stores(i * TOGETHER + b):
                copy.start()

    @pl.loop(heads - SLOTS, heads)
    def _(h):
        for copy in stores(h):
            copy.wait()

    for copy in wholes:
        copy.wait()


def on_device(side, queries, key_rows, value_rows, out_grad):
    heads, length, width = queries.shape
    chunks = length // CHUNK
    row = pltpu.VMEM((heads, length, width), HALF)
    part = pltpu.VMEM((heads, length, width), WIDE)
    inner = pltpu.VMEM((heads, chunks - 1, width, width), WIDE)
    state = pltpu.VMEM((heads, width, width), HALF)
    vmem = pl.BlockSpec(memory_space=pltpu.VMEM)
    hbm = pl.BlockSpec(memory_space=pl.ANY)
    held = pl.pallas_call(
        functools.partial(states_kernel, side),
        out_shape=[row] * 4 + [part] * 2 + [inner, state],
        in_specs=[hbm] * 4,
        out_specs=[vmem] * 8,
        scratch_shapes=[row] * 2
        + [part] * 2
        + [inner, state, pltpu.VMEM((length, width), WIDE)]
        + [pltpu.VMEM((2, heads, width, width), HALF)] * 3
        + [
            pltpu.SemaphoreType.DMA((2, 2, side)),
            pltpu.SemaphoreType.DMA((2, 2)),
            pltpu.SemaphoreType.DMA((2, 2)),
        ],
        compiler_params=pltpu.CompilerParams(collective_id=0, has_side_effects=True, vmem_limit_bytes=26 * 2**20),
        name="states",
    )(queries, key_rows, value_rows, out_grad)
    return pl.pallas_call(
        finish_kernel,
        out_shape=[jax.ShapeDtypeStruct((heads, length, width), HALF)] * 4,
        in_specs=[vmem] * 8,
        out_specs=[hbm] * 4,
        scratch_shapes=[pltpu.VMEM((SLOTS, length, width), HALF)] * 2
        + [pltpu.SemaphoreType.DMA((2,)), pltpu.SemaphoreType.DMA((2, SLOTS))],
        compiler_params=pltpu.CompilerParams(vmem_limit_bytes=8 * 2**20),
        name="finish",
    )(*held)


def solution(mesh):
    side = 4
    placed = P(None, ("dp", "seq"), None)
    return jax.shard_map(
        functools.partial(on_device, side),
        mesh=mesh,
        in_specs=(placed,) * 4,
        out_specs=(placed,) * 4,
        check_vma=False,
    )
```
